32 devices in a mesh: seq: 8 (over z, y), head: 4 (over x, core).
Axes of the slice: x: 2, y: 2, z: 4, core: 2. Of those that a mesh axis runs over, the one named last changes fastest.
Arguments:
- tokens: bfloat16 [4096, 3072], P(('seq', 'head')), may hold values from -6 to 6
- owner_shard: int32 [4096, 1], P(('seq', 'head')), may hold values from 0 to 7; in each aligned block of 128 rows (0 to 127, 128 to 255, ...) at most 48 rows name the same one
- dest_slot: int32 [4096], P(('seq', 'head')), may hold values from 0 to 127
- w_qkv: bfloat16 [3072, 3, 1536], P(None, None, 'head'), may hold values from -0.109375 to 0.109375
- w_out: bfloat16 [1536, 3072], P('head'), may hold values from -3 to 3
- norm_gain: float32 [3072], replicated, may hold values from 0.5 to 1.5
- norm_shift: float32 [3072], replicated, may hold values from -3 to 3
- query_gain: float32 [128], replicated, may hold values from 0.5 to 16
- key_gain: float32 [128], replicated, may hold values from 0.5 to 16
- out_gate: float32 [3072], replicated, may hold values from 0.5 to 2
Outputs:
- unmerged: bfloat16 [4096, 3072], P(('seq', 'head'))
The draws below stay inside these ranges and needn't reach their ends.
Inputs may be any that keep to these rules, and one draw needn't show every extreme that they name: `owner_shard`: among the rows of one device at most 48 name the same owner, a bound that some block reaches of them on some or all devices.
All inputs are finite; a program needn't handle non-finite values.
Results may differ from the reference program's by a relative error of at most 0.01195.
The reference program's roundings to bfloat16 on the way (of `normed`, `queries`, `keys_all`, `values_all`, `expweights`, `attended` and `merged_out`) count: a program that leaves them out, or rounds other values in their place, can miss the bound.
Values may be sent and summed in bfloat16 or wider, within the bound.
A program may use at most 128 MiB of HBM per device.

```python
import math
import jax
import jax.numpy as jnp
import numpy as np
from jax import lax

D = 3072
HDIM = 128
SRC_DEV = 128
HEADS = 12
TOKENS = 4096
MRG_SEQ = 128
MERGED = 1024
CAP = 48
N_SEQ = 8


def spread_gain(key, salt_number):
    lower_end = math.log(0.5)
    upper_end = math.log(2.0)
    baseline = jnp.exp(jax.random.uniform(jax.random.fold_in(key, salt_number), (HDIM,), jnp.float32, lower_end, upper_end))
    return baseline


def draw_query_gain(key, part):
    return spread_gain(key, 11)


def draw_key_gain(key, part):
    return spread_gain(key, 23)


def place_ends(array, own_key, smallest, high):
    spot = [jax.random.randint(jax.random.fold_in(own_key, axis), (), 0, length) for axis, length in enumerate(array.shape)]
    longest = array.shape.index(max(array.shape))
    beside = spot[:longest] + [(spot[longest] + 1) % array.shape[longest]] + spot[longest + 1:]
    return array.at[tuple(spot)].set(smallest).at[tuple(beside)].set(high)


def levels(rng, dims, shards, least, top_value):
    def one(dim, blocks):
        heights = jax.random.uniform(jax.random.fold_in(jax.random.fold_in(rng, 6), dim), (blocks,), jnp.float32, least / len(shards), top_value / len(shards))
        return jnp.repeat(jnp.exp(heights), dims[dim] // blocks).reshape((-1,) + (1,) * (len(dims) - dim - 1))

    loudness = one(*shards[0])
    for cut in shards[1:]:
        loudness = loudness * one(*cut)
    return loudness


def routed_block(key, own, number, rows, count, top, most, lean):
    order = jax.random.permutation(key, count)
    crowded, usual = load_shares(count, rows * top, most, lean, True), load_shares(count, rows * top, most, lean, False)
    places = jnp.arange(count)

    def named(lengths, offset_by):
        used = int((lengths > 0).sum())
        fixed = max(1, used // 4)
        shifted = fixed + (places - fixed + offset_by * (used - fixed)) % max(1, count - fixed)
        return jnp.zeros((count,), jnp.int32).at[order[jnp.where(places < fixed, places, shifted)]].set(jnp.asarray(lengths, jnp.int32))

    lengths = jnp.where(number % 4 == 0, named(crowded, number // 4), named(usual, number - number // 4 - 1))
    mixed = jax.random.permutation(jax.random.fold_in(own, 3), count)
    giver, taker = mixed[0:count // 2 * 2:2], mixed[1:count // 2 * 2:2]
    room = jnp.minimum(lengths[giver] - 1, most - lengths[taker]) // 2
    room = jnp.where((giver == order[0]) | (taker == order[0]) | (lengths[taker] == 0), 0, jnp.maximum(room, 0))
    shifted = jax.random.randint(jax.random.fold_in(own, 4), (count // 2,), 0, 1 << 20) % (room + 1)
    lengths = lengths.at[giver].add(-shifted).at[taker].add(shifted)
    labels = jnp.searchsorted(jnp.cumsum(lengths), jnp.arange(rows * top), side="right").astype(jnp.int32)
    grid = labels.reshape(top, rows).T
    grid = grid[jax.random.permutation(jax.random.fold_in(own, 1), rows)]
    offset_by = jax.random.randint(jax.random.fold_in(own, 2), (rows, 1), 0, top)
    return jnp.take_along_axis(grid, (jnp.arange(top)[None, :] + offset_by) % top, axis=1)


def load_shares(amount, total, reach, lean, full):
    weights = [(1 << 20) // math.isqrt(grade ** lean) + 1 for grade in range(1, amount + 1)]
    largest = reach if full else min(reach, max(-(-total // amount), total * weights[0] // sum(weights)))
    least = 1 if total - largest >= amount - 1 else 0
    counts, spare = [largest] + [least] * (amount - 1), total - largest - least * (amount - 1)
    while spare > 0:
        candidates = [i for i in range(1, amount) if counts[i] < largest] or [i for i in range(1, amount) if counts[i] < reach]
        pool, budget = sum([weights[i] for i in candidates]), spare
        for i in candidates:
            more = min(reach - counts[i], max(1, budget * weights[i] // pool), spare)
            counts[i] = counts[i] + more
            spare = spare - more
    return np.array(counts)


def scatter_about(key, dims, scale, bound, split=(), dtype=jnp.bfloat16):
    entries = jax.random.normal(key, dims, jnp.float32) * scale
    if len(split) > 0:
        entries = levels(key, dims, split, -0.22, 0.18) * entries
    return jnp.clip(entries, min=-bound, max=bound).astype(dtype)


def setup_inputs(seed: int = 0) -> dict:
    key_of = jax.random.split(jax.random.key(seed), 11)
    tokens = scatter_about(key_of[0], (TOKENS, D), 1.0, 6.0, ((0, 32),))
    owner_shard_keys = jax.random.split(jax.random.fold_in(key_of[1], 1), TOKENS // SRC_DEV)
    owner_shard_turns = jax.random.permutation(jax.random.fold_in(key_of[1], 3), TOKENS // SRC_DEV)
    owner_shard = jax.vmap(lambda own, number: routed_block(jax.random.fold_in(key_of[1], 2), own, number, SRC_DEV, N_SEQ, 1, CAP, 2))(owner_shard_keys, owner_shard_turns).reshape((TOKENS, 1))
    dest_slot = place_ends(jax.random.randint(key_of[2], (TOKENS,), 0, MRG_SEQ), jax.random.fold_in(key_of[2], 1), 0, MRG_SEQ - 1).astype(jnp.int32)
    w_qkv = scatter_about(key_of[3], (D, 3, HEADS * HDIM), D ** -0.5, 0.109375, ((2, 4),))
    w_out = scatter_about(key_of[4], (HEADS * HDIM, D), 0.5, 3.0, ((0, 4),))
    norm_gain = jnp.clip(jax.random.uniform(key_of[5], (D,), jnp.float32, 0.5, 1.5), 0.5, 1.5)
    norm_shift = scatter_about(key_of[6], (D,), 0.5, 3.0, (), jnp.float32)
    query_gain = draw_query_gain(jax.random.fold_in(key_of[10], 71), 0)
    key_gain = draw_key_gain(jax.random.fold_in(key_of[10], 71), 0)
    out_gate = jnp.clip(jax.random.uniform(key_of[9], (D,), jnp.float32, 0.5, 2.0), 0.5, 2.0)
    return {"tokens": tokens, "owner_shard": owner_shard, "dest_slot": dest_slot, "w_qkv": w_qkv, "w_out": w_out, "norm_gain": norm_gain, "norm_shift": norm_shift, "query_gain": query_gain, "key_gain": key_gain, "out_gate": out_gate}


def rms_scale(values_in):
    return values_in * lax.rsqrt(lax.optimization_barrier(jnp.mean(values_in * values_in, -1, keepdims=True)) + 1e-06)

def reference(tokens, owner_shard, dest_slot, w_qkv, w_out, norm_gain, norm_shift, query_gain, key_gain, out_gate):
    destination = (owner_shard[:, 0] * MRG_SEQ + dest_slot).astype(jnp.int32)
    merged_sums = jax.ops.segment_sum(tokens.astype(jnp.float32), destination, num_segments=MERGED)
    row_mean = lax.optimization_barrier(jnp.mean(merged_sums, -1, keepdims=True))
    centered = merged_sums - row_mean
    row_var = lax.optimization_barrier(jnp.mean(centered * centered, -1, keepdims=True))
    normed = (centered * lax.rsqrt(row_var + 1e-06) * norm_gain + norm_shift).astype(jnp.bfloat16)
    projected = jnp.dot(normed, w_qkv.reshape(D, 3 * HEADS * HDIM), preferred_element_type=jnp.float32)
    projected = projected.reshape(MERGED, 3, HEADS, HDIM)
    queries = (rms_scale(projected[:, 0]) * query_gain / math.sqrt(HDIM)).astype(jnp.bfloat16)
    keys_all = (rms_scale(projected[:, 1]) * key_gain).astype(jnp.bfloat16).astype(jnp.float32)
    values_all = projected[:, 2].astype(jnp.bfloat16).astype(jnp.float32)

    def attend_block(query_block):
        scores = jnp.einsum('qhd,khd->hqk', query_block.astype(jnp.float32), keys_all)
        row_peak = lax.optimization_barrier(jnp.max(scores, -1, keepdims=True))
        expo = jnp.exp(scores - row_peak)
        denominator = lax.optimization_barrier(jnp.sum(expo, -1))
        expweights = lax.optimization_barrier(expo.astype(jnp.bfloat16)).astype(jnp.float32)
        numerator = jnp.einsum('hqk,khd->qhd', expweights, values_all)
        return (numerator / jnp.transpose(denominator)[:, :, None]).astype(jnp.bfloat16)
    blocks = queries.reshape(MERGED // 256, 256, HEADS, HDIM)
    attended = lax.map(attend_block, blocks).reshape(MERGED, HEADS * HDIM)
    merged_out = (jnp.dot(attended, w_out, preferred_element_type=jnp.float32) * out_gate).astype(jnp.bfloat16)
    return jnp.take(merged_out, destination, axis=0)
```

```python
import functools
import math

import jax
import jax.numpy as jnp
from jax import lax
from jax.experimental import pallas as pl
from jax.experimental.pallas import tpu as pltpu
from jax.sharding import PartitionSpec as P

HDIM = 128
RATIO = 4
MESH = pl.DeviceIdType.MESH
ANY = pl.BlockSpec(memory_space=pl.ANY)


def rms_scale(values_in):
    return values_in * lax.rsqrt(jnp.mean(values_in * values_in, -1, keepdims=True) + 1e-06)


def plane_width(seq_count):
    return 2 if seq_count % 2 == 0 else 1


class Plane:
    def __init__(self, seq_count, head_count):
        self.wide = plane_width(seq_count)
        self.heads = head_count
        self.size = self.wide * head_count

    def me(self):
        return lax.rem(lax.axis_index("seq"), self.wide) * self.heads + lax.axis_index("head")

    def device(self, index):
        base = lax.axis_index("seq") // self.wide * self.wide
        return (base + index // self.heads, lax.rem(index, self.heads))


class Line:
    def __init__(self, seq_count, head_count):
        self.wide = plane_width(seq_count)
        self.size = seq_count // self.wide

    def me(self):
        return lax.axis_index("seq") // self.wide

    def device(self, index):
        return (index * self.wide + lax.rem(lax.axis_index("seq"), self.wide), lax.axis_index("head"))


def greet(devices):
    barrier = pltpu.get_barrier_semaphore()
    for device in devices:
        pl.semaphore_signal(barrier, inc=1, device_id=device, device_id_type=MESH)
    pl.semaphore_wait(barrier, len(devices))


def exchange_kernel(group, count, source_of, target_of, *refs):
    sources, targets = refs[:count], refs[count : 2 * count]
    send_sem, recv_sem, own_sem = refs[2 * count :]
    size, me = group.size, group.me()
    others = [lax.rem(me + step, size) for step in range(1, size)]
    greet([group.device(other) for other in others])
    copies = []
    for step, other in enumerate(others):
        for item in range(count):
            copy = pltpu.make_async_remote_copy(
                src_ref=source_of[item](sources[item], other),
                dst_ref=target_of[item](targets[item], me),
                send_sem=send_sem.at[item, step],
                recv_sem=recv_sem.at[item, step],
                device_id=group.device(other),
                device_id_type=MESH,
            )
            copy.start()
            copies.append(copy)
    for item in range(count):
        own = pltpu.make_async_copy(
            source_of[item](sources[item], me), target_of[item](targets[item], me), own_sem.at[item]
        )
        own.start()
        copies.append(own)
    for copy in copies:
        copy.wait()


def exchange(number, group, arrays, shapes, source_of, target_of):
    count = len(arrays)
    return pl.pallas_call(
        functools.partial(exchange_kernel, group, count, source_of, target_of),
        out_shape=[
            jax.ShapeDtypeStruct(shape, array.dtype) for shape, array in zip(shapes, arrays)
        ],
        in_specs=[ANY] * count,
        out_specs=[ANY] * count,
        scratch_shapes=[
            pltpu.SemaphoreType.DMA((count, group.size - 1)),
            pltpu.SemaphoreType.DMA((count, group.size - 1)),
            pltpu.SemaphoreType.DMA((count,)),
        ],
        compiler_params=pltpu.CompilerParams(collective_id=number, has_side_effects=True),
        name="exchange_" + str(number),
    )(*arrays)


def whole(ref, index):
    return ref


def block(ref, index):
    return ref.at[index]


def columns(width, ref, index):
    return ref.at[:, pl.ds(pl.multiple_of(index * width, width), width)]


def gather_kernel(wide, length, count, *refs):
    sources, targets = refs[:count], refs[count : 2 * count]
    line_send, line_recv, side_send, side_recv, own_sem = refs[2 * count :]
    seq, head = lax.axis_index("seq"), lax.axis_index("head")
    z, y = seq // wide, lax.rem(seq, wide)
    beside = [z * wide + lax.rem(y + turn, wide) for turn in range(1, wide)]
    along = [lax.rem(z + step, length) for step in range(1, length)]
    greet([(z * wide + lax.rem(y + turn, wide), head) for turn in range(1, wide)]
          + [(other * wide + y, head) for other in along])
    copies, arriving = [], []

    def remote(source, target, send, recv, device):
        copy = pltpu.make_async_remote_copy(
            src_ref=source, dst_ref=target, send_sem=send, recv_sem=recv,
            device_id=device, device_id_type=MESH,
        )
        copy.start()
        return copy

    for step, other in enumerate(along):
        for item in range(count):
            arriving.append(remote(
                sources[item], targets[item].at[seq], line_send.at[item, step],
                line_recv.at[item, step], (other * wide + y, head)))
    for turn, other in enumerate(beside):
        for item in range(count):
            copies.append(remote(
                sources[item], targets[item].at[seq], side_send.at[item, turn, 0],
                side_recv.at[item, turn, 0], (other, head)))
    for item in range(count):
        own = pltpu.make_async_copy(sources[item], targets[item].at[seq], own_sem.at[item])
        own.start()
        copies.append(own)
    for step in range(length - 1):
        come = lax.rem(z + length - 1 - step, length) * wide + y
        for item in range(count):
            arriving[step * count + item].wait_recv()
            for turn, other in enumerate(beside):
                copies.append(remote(
                    targets[item].at[come], targets[item].at[come],
                    side_send.at[item, turn, step + 1], side_recv.at[item, turn, step + 1],
                    (other, head)))
    for copy in arriving:
        copy.wait_send()
    for copy in copies:
        copy.wait()


def gather_seq(number, seq_count, arrays):
    wide = plane_width(seq_count)
    length, count = seq_count // wide, len(arrays)
    return pl.pallas_call(
        functools.partial(gather_kernel, wide, length, count),
        out_shape=[jax.ShapeDtypeStruct((seq_count, *a.shape), a.dtype) for a in arrays],
        in_specs=[ANY] * count,
        out_specs=[ANY] * count,
        scratch_shapes=[
            pltpu.SemaphoreType.DMA((count, length)),
            pltpu.SemaphoreType.DMA((count, length)),
            pltpu.SemaphoreType.DMA((count, wide, length)),
            pltpu.SemaphoreType.DMA((count, wide, length)),
            pltpu.SemaphoreType.DMA((count,)),
        ],
        compiler_params=pltpu.CompilerParams(collective_id=number, has_side_effects=True),
        name="gather_" + str(number),
    )(*arrays)


def on_device(
    tokens,
    owner_shard,
    dest_slot,
    w_qkv,
    w_out,
    norm_gain,
    norm_shift,
    query_gain,
    key_gain,
    out_gate,
):
    seq_count = lax.axis_size("seq")
    head_count = lax.axis_size("head")
    src_rows, feature_width = tokens.shape
    merged_rows = src_rows * head_count // RATIO
    plane, line = Plane(seq_count, head_count), Line(seq_count, head_count)
    wide = plane.wide
    part = feature_width // plane.size
    own_columns = functools.partial(columns, part)
    first_column = plane.me() * part
    plane_tokens = plane.size * src_rows
    plane_rows = wide * merged_rows

    destination = (owner_shard[:, 0] * merged_rows + dest_slot)[None, :]
    seen, seen_ids = exchange(
        0,
        plane,
        [tokens, destination],
        [(plane.size, src_rows, part), (plane.size, 1, src_rows)],
        [own_columns, whole],
        [block, block],
    )
    seen = seen.reshape(plane_tokens, part)
    seen_ids = seen_ids.reshape(plane_tokens)
    selector = jnp.arange(seq_count * merged_rows, dtype=jnp.int32)[:, None] == seen_ids[None, :]
    partial_sums = jnp.dot(selector.astype(jnp.bfloat16), seen, preferred_element_type=jnp.float32)
    [gathered] = exchange(
        1,
        line,
        [partial_sums.reshape(line.size, plane_rows, part)],
        [(line.size, plane_rows, part)],
        [block],
        [block],
    )
    sums = jnp.sum(gathered, 0)
    part_mean = jnp.mean(sums, -1)
    part_spread = jnp.sum((sums - part_mean[:, None]) ** 2, -1)
    [stats] = exchange(
        2,
        plane,
        [jnp.stack([part_mean, part_spread])],
        [(plane.size, 2, plane_rows)],
        [whole],
        [block],
    )
    row_mean = jnp.mean(stats[:, 0], 0)
    apart = stats[:, 0] - row_mean[None, :]
    row_var = (jnp.sum(stats[:, 1], 0) + part * jnp.sum(apart * apart, 0)) / feature_width

    def own_part(vector):
        return lax.dynamic_slice(vector, (first_column,), (part,))

    normed = (
        (sums - row_mean[:, None]) * lax.rsqrt(row_var + 1e-06)[:, None] * own_part(norm_gain)
        + own_part(norm_shift)
    ).astype(jnp.bfloat16)
    [normed] = exchange(
        3,
        plane,
        [normed.reshape(wide, merged_rows, part)],
        [(merged_rows, feature_width)],
        [lambda ref, index: ref.at[index // head_count]],
        [own_columns],
    )
    head_width = w_qkv.shape[2]
    local_heads = head_width // HDIM
    weights = jnp.transpose(w_qkv, (1, 0, 2))

    def projected(which):
        return jnp.dot(normed, weights[which], preferred_element_type=jnp.float32)

    def by_head(values_in):
        return values_in.reshape(merged_rows, local_heads, HDIM)

    queries = (rms_scale(by_head(projected(0))) * query_gain / math.sqrt(HDIM)).astype(jnp.bfloat16)
    keys_local = (rms_scale(by_head(projected(1))) * key_gain).astype(jnp.bfloat16)
    values_local = projected(2).astype(jnp.bfloat16)
    keys_all, values_all = gather_seq(
        4,
        seq_count,
        [keys_local.reshape(merged_rows, head_width), values_local],
    )
    keys_all = keys_all.reshape(-1, local_heads, HDIM)
    values_all = values_all.reshape(-1, local_heads, HDIM)
    scores = jnp.einsum("qhd,khd->hqk", queries, keys_all, preferred_element_type=jnp.float32)
    expweights = jnp.exp(scores - jnp.max(scores, -1, keepdims=True))
    total = jnp.sum(expweights, -1)
    weighted = jnp.einsum(
        "hqk,khd->qhd",
        expweights.astype(jnp.bfloat16),
        values_all,
        preferred_element_type=jnp.float32,
    )
    attended = (weighted / jnp.transpose(total)[:, :, None]).astype(jnp.bfloat16)
    attended = attended.reshape(merged_rows, head_width)
    partial_out = jnp.dot(attended, w_out, preferred_element_type=jnp.float32).astype(jnp.bfloat16)
    [pieces] = exchange(
        5,
        plane,
        [partial_out],
        [(plane.size, merged_rows, part)],
        [own_columns],
        [block],
    )
    pieces = pieces.reshape(wide, head_count, merged_rows, part).astype(jnp.float32)
    merged_out = (jnp.sum(pieces, 1) * own_part(out_gate)).astype(jnp.bfloat16)
    [merged_all] = exchange(
        6,
        line,
        [merged_out.reshape(plane_rows, part)],
        [(line.size, plane_rows, part)],
        [whole],
        [block],
    )
    merged_all = merged_all.reshape(seq_count * merged_rows, part)
    chooser = seen_ids[:, None] == jnp.arange(seq_count * merged_rows, dtype=jnp.int32)[None, :]
    fetched = jnp.dot(
        chooser.astype(jnp.bfloat16), merged_all, preferred_element_type=jnp.float32
    ).astype(jnp.bfloat16)
    [returned] = exchange(
        7,
        plane,
        [fetched.reshape(plane.size, src_rows, part)],
        [(src_rows, feature_width)],
        [block],
        [own_columns],
    )
    return returned


def solution(mesh):
    placed = (
        P(("seq", "head"), None),
        P(("seq", "head"), None),
        P(("seq", "head")),
        P(None, None, "head"),
        P("head", None),
        P(),
        P(),
        P(),
        P(),
        P(),
    )
    return jax.shard_map(
        on_device, mesh=mesh, in_specs=placed, out_specs=P(("seq", "head"), None), check_vma=False
    )
```

```python
import functools
import math

import jax
import jax.numpy as jnp
from jax import lax
from jax.experimental import pallas as pl
from jax.experimental.pallas import tpu as pltpu
from jax.sharding import PartitionSpec as P

HDIM = 128
RATIO = 4
MESH = pl.DeviceIdType.MESH
ANY = pl.BlockSpec(memory_space=pl.ANY)


def rms_scale(values_in):
    return values_in * lax.rsqrt(jnp.mean(values_in * values_in, -1, keepdims=True) + 1e-06)


def plane_width(seq_count):
    return 2 if seq_count % 2 == 0 else 1


class Plane:
    def __init__(self, seq_count, head_count):
        self.wide = plane_width(seq_count)
        self.heads = head_count
        self.size = self.wide * head_count

    def me(self):
        return lax.rem(lax.axis_index("seq"), self.wide) * self.heads + lax.axis_index("head")

    def device(self, index):
        base = lax.axis_index("seq") // self.wide * self.wide
        return (base + index // self.heads, lax.rem(index, self.heads))


class Line:
    def __init__(self, seq_count, head_count):
        self.wide = plane_width(seq_count)
        self.size = seq_count // self.wide

    def me(self):
        return lax.axis_index("seq") // self.wide

    def device(self, index):
        return (index * self.wide + lax.rem(lax.axis_index("seq"), self.wide), lax.axis_index("head"))


def greet(devices):
    barrier = pltpu.get_barrier_semaphore()
    for device in devices:
        pl.semaphore_signal(barrier, inc=1, device_id=device, device_id_type=MESH)
    pl.semaphore_wait(barrier, len(devices))


def exchange_kernel(group, count, source_of, target_of, *refs):
    sources, targets = refs[:count], refs[count : 2 * count]
    send_sem, recv_sem, own_sem = refs[2 * count :]
    size, me = group.size, group.me()
    others = [lax.rem(me + step, size) for step in range(1, size)]
    greet([group.device(other) for other in others])
    copies = []
    for step, other in enumerate(others):
        for item in range(count):
            copy = pltpu.make_async_remote_copy(
                src_ref=source_of[item](sources[item], other),
                dst_ref=target_of[item](targets[item], me),
                send_sem=send_sem.at[item, step],
                recv_sem=recv_sem.at[item, step],
                device_id=group.device(other),
                device_id_type=MESH,
            )
            copy.start()
            copies.append(copy)
    for item in range(count):
        own = pltpu.make_async_copy(
            source_of[item](sources[item], me), target_of[item](targets[item], me), own_sem.at[item]
        )
        own.start()
        copies.append(own)
    for copy in copies:
        copy.wait()


def exchange(number, group, arrays, shapes, source_of, target_of):
    count = len(arrays)
    return pl.pallas_call(
        functools.partial(exchange_kernel, group, count, source_of, target_of),
        out_shape=[
            jax.ShapeDtypeStruct(shape, array.dtype) for shape, array in zip(shapes, arrays)
        ],
        in_specs=[ANY] * count,
        out_specs=[ANY] * count,
        scratch_shapes=[
            pltpu.SemaphoreType.DMA((count, group.size - 1)),
            pltpu.SemaphoreType.DMA((count, group.size - 1)),
            pltpu.SemaphoreType.DMA((count,)),
        ],
        compiler_params=pltpu.CompilerParams(collective_id=number, has_side_effects=True),
        name="exchange_" + str(number),
    )(*arrays)


def whole(ref, index):
    return ref


def block(ref, index):
    return ref.at[index]


def columns(width, ref, index):
    return ref.at[:, pl.ds(pl.multiple_of(index * width, width), width)]


def gather_kernel(wide, length, count, *refs):
    sources, targets = [ref.at[pl.ds(1, 2)] for ref in refs[:count]], refs[count : 2 * count]
    line_send, line_recv, side_send, side_recv, own_sem = refs[2 * count :]
    seq, head = lax.axis_index("seq"), lax.axis_index("head")
    z, y = seq // wide, lax.rem(seq, wide)
    beside = [z * wide + lax.rem(y + turn, wide) for turn in range(1, wide)]
    along = [lax.rem(z + step, length) for step in range(1, length)]
    greet([(z * wide + lax.rem(y + turn, wide), head) for turn in range(1, wide)]
          + [(other * wide + y, head) for other in along])
    copies, arriving = [], []

    def begin(*ends):
        copy = remote(*ends)
        copy.start()
        return copy

    for step, other in enumerate(along):
        for item in range(count):
            arriving.append(begin(
                sources[item], targets[item].at[seq], line_send.at[item, step],
                line_recv.at[item, step], (other * wide + y, head)))
    for turn, other in enumerate(beside):
        for item in range(count):
            copies.append(begin(
                sources[item], targets[item].at[seq], side_send.at[item, turn, 0],
                side_recv.at[item, turn, 0], (other, head)))
    for item in range(count):
        own = pltpu.make_async_copy(sources[item], targets[item].at[seq], own_sem.at[item])
        own.start()
        copies.append(own)
    for step in range(length - 1):
        come = lax.rem(z + length - 1 - step, length) * wide + y
        for item in range(count):
            arriving[step * count + item].wait_recv()
            for turn, other in enumerate(beside):
                copies.append(begin(
                    targets[item].at[come], targets[item].at[come],
                    side_send.at[item, turn, step + 1], side_recv.at[item, turn, step + 1],
                    (other, head)))
    for copy in arriving:
        copy.wait_send()
    for copy in copies:
        copy.wait()


def gather_seq(number, seq_count, arrays):
    wide = plane_width(seq_count)
    length, count = seq_count // wide, len(arrays)
    return pl.pallas_call(
        functools.partial(gather_kernel, wide, length, count),
        out_shape=[jax.ShapeDtypeStruct((seq_count, 2, *a.shape[1:]), a.dtype) for a in arrays],
        in_specs=[ANY] * count,
        out_specs=[ANY] * count,
        scratch_shapes=[
            pltpu.SemaphoreType.DMA((count, length)),
            pltpu.SemaphoreType.DMA((count, length)),
            pltpu.SemaphoreType.DMA((count, wide, length)),
            pltpu.SemaphoreType.DMA((count, wide, length)),
            pltpu.SemaphoreType.DMA((count,)),
        ],
        compiler_params=pltpu.CompilerParams(collective_id=number, has_side_effects=True),
        name="gather_" + str(number),
    )(*arrays)


LANES = 128
VMEM = pl.BlockSpec(memory_space=pltpu.VMEM)


def remote(source, target, send, recv, device):
    return pltpu.make_async_remote_copy(
        src_ref=source, dst_ref=target, send_sem=send, recv_sem=recv,
        device_id=device, device_id_type=MESH,
    )


def to_row(column):
    return jnp.transpose(jnp.broadcast_to(column, (column.shape[0], LANES)))[:8]


def to_column(row):
    return jnp.transpose(jnp.broadcast_to(row, (LANES, row.shape[1])))[:, :1]


def front_kernel(
    plane, line, chunks, tokens, ids, gain, shift, normed, all_ids, seen, part, passing, sums,
    stats, parts, id_send, id_recv, seen_send, seen_recv, pass_send, pass_recv, stat_send,
    stat_recv, norm_send, norm_recv, own_sem,
):
    me, z, length = plane.me(), line.me(), line.size
    src_rows = tokens.shape[0]
    rows = part.shape[2]
    width = chunks * LANES
    feature_width = width * plane.size
    others = [lax.rem(me + step, plane.size) for step in range(1, plane.size)]
    devices = [plane.device(other) for other in others]
    above, below = lax.rem(z + 1, length), lax.rem(z + length - 1, length)
    along = [lax.rem(z + step, length) for step in range(1, length)]
    greet(devices + [line.device(other) for other in along])

    def slab(index, chunk):
        return pl.ds(pl.multiple_of(index * width + chunk * LANES, LANES), LANES)

    started = []

    def go(copy):
        copy.start()
        started.append(copy)
        return copy

    id_copies = [
        go(remote(ids, all_ids.at[me], id_send.at[step], id_recv.at[step], device))
        for step, device in enumerate(devices)
    ]
    seen_copies = [
        [
            go(remote(tokens.at[:, slab(other, chunk)], seen.at[chunk, me],
                      seen_send.at[chunk, step], seen_recv.at[chunk, step], devices[step]))
            for step, other in enumerate(others)
        ]
        for chunk in range(chunks)
    ]
    all_ids[me] = ids[...]
    for chunk in range(chunks):
        seen[chunk, me] = tokens[:, slab(me, chunk)]
    for copy in id_copies:
        copy.wait_recv()
    labels = jnp.concatenate([all_ids[index] for index in range(plane.size)], axis=1)
    places = lax.broadcasted_iota(jnp.int32, (rows, 1), 0)

    def upward(chunk, dest):
        return remote(part.at[chunk, dest], passing.at[chunk, dest + 1], pass_send.at[chunk, dest + 1],
                      pass_recv.at[chunk, dest + 1], line.device(above))

    def downward(chunk, dest):
        return remote(part.at[chunk, dest], passing.at[chunk, dest], pass_send.at[chunk, dest],
                      pass_recv.at[chunk, dest], line.device(below))

    for chunk in range(chunks):
        for copy in seen_copies[chunk]:
            copy.wait_recv()
        arrived = seen[chunk].reshape(plane.size * src_rows, LANES)
        for dest in range(length):
            chosen = (places + dest * rows == labels).astype(jnp.float32).astype(jnp.bfloat16)
            part[chunk, dest] = jnp.dot(chosen, arrived, preferred_element_type=jnp.float32)
        for turn in range(length - 1):
            high, low = length - 1 - turn, turn

            @pl.when(z < high)
            def _():
                @pl.when(z > 0)
                def _():
                    upward(chunk, high).wait_recv()
                    part[chunk, high] += passing[chunk, high + 1]
                upward(chunk, high).start()

            @pl.when(z > low)
            def _():
                @pl.when(z < length - 1)
                def _():
                    downward(chunk, low).wait_recv()
                    part[chunk, low] += passing[chunk, low]
                downward(chunk, low).start()

    for chunk in range(chunks):
        for dest in range(length):
            @pl.when(z == dest)
            def _():
                total = part[chunk, dest]
                if dest > 0:
                    upward(chunk, dest).wait_recv()
                    total = total + passing[chunk, dest + 1]
                if dest < length - 1:
                    downward(chunk, dest).wait_recv()
                    total = total + passing[chunk, dest]
                sums[:, chunk * LANES:(chunk + 1) * LANES] = total

    values = sums[...]
    part_mean = jnp.mean(values, -1, keepdims=True)
    apart = values - part_mean
    spread = jnp.sum(apart * apart, -1, keepdims=True)
    stats[me, 0:8] = to_row(part_mean)
    stats[me, 8:16] = to_row(spread)
    stat_copies = [
        go(remote(stats.at[me], stats.at[me], stat_send.at[step], stat_recv.at[step], device))
        for step, device in enumerate(devices)
    ]
    for copy in stat_copies:
        copy.wait_recv()
    means = [stats[index, 0:1] for index in range(plane.size)]
    row_mean = sum(means) * (1.0 / plane.size)
    row_var = sum([stats[index, 8:9] for index in range(plane.size)])
    for mean in means:
        row_var = row_var + width * (mean - row_mean) * (mean - row_mean)
    scale = to_column(lax.rsqrt(row_var * (1.0 / feature_width) + 1e-06))
    own = pl.ds(pl.multiple_of(me * width, LANES), width)
    parts[...] = (
        (values - to_column(row_mean)) * scale * gain[:, own] + shift[:, own]
    ).astype(jnp.bfloat16)
    merged_rows = rows // plane.wide

    def rows_of(index):
        return pl.ds(pl.multiple_of(index // plane.heads * merged_rows, merged_rows), merged_rows)

    norm_copies = [
        go(remote(parts.at[rows_of(other)], normed.at[:, own], norm_send.at[step],
                  norm_recv.at[step], devices[step]))
        for step, other in enumerate(others)
    ]
    mine = pltpu.make_async_copy(parts.at[rows_of(me)], normed.at[:, own], own_sem)
    mine.start()
    mine.wait()
    for copy in norm_copies:
        copy.wait_recv()
    for copy in started:
        copy.wait_send()
    for chunk in range(chunks):
        for dest in range(length):
            @pl.when(z < dest)
            def _():
                upward(chunk, dest).wait_send()

            @pl.when(z > dest)
            def _():
                downward(chunk, dest).wait_send()


def front(number, plane, line, tokens, ids, gain, shift):
    src_rows, feature_width = tokens.shape
    width = feature_width // plane.size
    chunks = width // LANES
    merged_rows = src_rows * plane.heads // RATIO
    rows = plane.wide * merged_rows
    dma = pltpu.SemaphoreType.DMA
    others = plane.size - 1
    return pl.pallas_call(
        functools.partial(front_kernel, plane, line, chunks),
        out_shape=[
            jax.ShapeDtypeStruct((merged_rows, feature_width), jnp.bfloat16),
            jax.ShapeDtypeStruct((plane.size, 1, src_rows), jnp.int32),
        ],
        in_specs=[VMEM] * 4,
        out_specs=[VMEM] * 2,
        scratch_shapes=[
            pltpu.VMEM((chunks, plane.size, src_rows, LANES), jnp.bfloat16),
            pltpu.VMEM((chunks, line.size, rows, LANES), jnp.float32),
            pltpu.VMEM((chunks, line.size + 1, rows, LANES), jnp.float32),
            pltpu.VMEM((rows, width), jnp.float32),
            pltpu.VMEM((plane.size, 16, rows), jnp.float32),
            pltpu.VMEM((rows, width), jnp.bfloat16),
            dma((others,)),
            dma((others,)),
            dma((chunks, others)),
            dma((chunks, others)),
            dma((chunks, line.size + 1)),
            dma((chunks, line.size + 1)),
            dma((others,)),
            dma((others,)),
            dma((others,)),
            dma((others,)),
            dma(()),
        ],
        compiler_params=pltpu.CompilerParams(
            collective_id=number, has_side_effects=True, vmem_limit_bytes=56 * 2**20
        ),
        name="front",
    )(tokens, ids, gain, shift)


def project_kernel(normed, weights, gains, out):
    made = jnp.dot(normed[...], weights[0], preferred_element_type=jnp.float32)
    plain = pl.program_id(0) == 2
    for start in range(0, made.shape[1], HDIM):
        one = made[:, start:start + HDIM]
        scaled = rms_scale(one) * gains[0]
        out[0, :, start:start + HDIM] = jnp.where(plain, one, scaled).astype(jnp.bfloat16)


def project(normed, weights, gains):
    rows, depth = normed.shape
    width = weights.shape[2]
    return pl.pallas_call(
        project_kernel,
        grid=(3,),
        out_shape=jax.ShapeDtypeStruct((3, rows, width), jnp.bfloat16),
        in_specs=[
            pl.BlockSpec((rows, depth), lambda j: (0, 0)),
            pl.BlockSpec((1, depth, width), lambda j: (j, 0, 0)),
            pl.BlockSpec((1, 1, HDIM), lambda j: (j, 0, 0)),
        ],
        out_specs=pl.BlockSpec((1, rows, width), lambda j: (j, 0, 0)),
        compiler_params=pltpu.CompilerParams(vmem_limit_bytes=56 * 2**20),
        name="project",
    )(normed, weights, gains)


def attend_kernel(mine, pairs, w_out, out):
    rows, width = mine.shape[1], mine.shape[2]
    heads = []
    for start in range(0, width, HDIM):
        spot = slice(start, start + HDIM)
        keys = pairs[:, 0, :, spot].reshape(-1, HDIM)
        values = pairs[:, 1, :, spot].reshape(-1, HDIM)
        scores = lax.dot_general(
            mine[0, :, spot], keys, (((1,), (1,)), ((), ())), preferred_element_type=jnp.float32
        )
        expo = jnp.exp(scores - jnp.max(scores, -1, keepdims=True))
        total = jnp.sum(expo, -1, keepdims=True)
        weighted = jnp.dot(expo.astype(jnp.bfloat16), values, preferred_element_type=jnp.float32)
        heads.append((weighted / total).astype(jnp.bfloat16))
    attended = jnp.concatenate(heads, axis=1)
    out[...] = jnp.dot(attended, w_out[...], preferred_element_type=jnp.float32).astype(jnp.bfloat16)


def attend(made, pairs, w_out):
    return pl.pallas_call(
        attend_kernel,
        out_shape=jax.ShapeDtypeStruct((made.shape[1], w_out.shape[1]), jnp.bfloat16),
        in_specs=[VMEM] * 3,
        out_specs=VMEM,
        compiler_params=pltpu.CompilerParams(vmem_limit_bytes=56 * 2**20),
        name="attend",
    )(made, pairs, w_out)


def on_device(
    tokens,
    owner_shard,
    dest_slot,
    w_qkv,
    w_out,
    norm_gain,
    norm_shift,
    query_gain,
    key_gain,
    out_gate,
):
    seq_count = lax.axis_size("seq")
    head_count = lax.axis_size("head")
    src_rows, feature_width = tokens.shape
    merged_rows = src_rows * head_count // RATIO
    plane, line = Plane(seq_count, head_count), Line(seq_count, head_count)
    wide = plane.wide
    part = feature_width // plane.size
    own_columns = functools.partial(columns, part)
    first_column = plane.me() * part
    plane_tokens = plane.size * src_rows
    plane_rows = wide * merged_rows

    destination = (owner_shard[:, 0] * merged_rows + dest_slot)[None, :]
    normed, seen_ids = front(0, plane, line, tokens, destination, norm_gain[None], norm_shift[None])
    seen_ids = seen_ids.reshape(plane_tokens)

    def own_part(vector):
        return lax.dynamic_slice(vector, (first_column,), (part,))

    gains = jnp.stack([query_gain / math.sqrt(HDIM), key_gain, jnp.ones_like(key_gain)])
    made = project(normed, jnp.transpose(w_qkv, (1, 0, 2)), gains[:, None])
    [pairs] = gather_seq(4, seq_count, [made])
    partial_out = attend(made, pairs, w_out)
    [pieces] = exchange(
        5,
        plane,
        [partial_out],
        [(plane.size, merged_rows, part)],
        [own_columns],
        [block],
    )
    pieces = pieces.reshape(wide, head_count, merged_rows, part).astype(jnp.float32)
    merged_out = (jnp.sum(pieces, 1) * own_part(out_gate)).astype(jnp.bfloat16)
    [merged_all] = exchange(
        6,
        line,
        [merged_out.reshape(plane_rows, part)],
        [(line.size, plane_rows, part)],
        [whole],
        [block],
    )
    merged_all = merged_all.reshape(seq_count * merged_rows, part)
    chooser = seen_ids[:, None] == jnp.arange(seq_count * merged_rows, dtype=jnp.int32)[None, :]
    fetched = jnp.dot(
        chooser.astype(jnp.bfloat16), merged_all, preferred_element_type=jnp.float32
    ).astype(jnp.bfloat16)
    [returned] = exchange(
        7,
        plane,
        [fetched.reshape(plane.size, src_rows, part)],
        [(src_rows, feature_width)],
        [block],
        [own_columns],
    )
    return returned


def solution(mesh):
    placed = (
        P(("seq", "head"), None),
        P(("seq", "head"), None),
        P(("seq", "head")),
        P(None, None, "head"),
        P("head", None),
        P(),
        P(),
        P(),
        P(),
        P(),
    )
    return jax.shard_map(
        on_device, mesh=mesh, in_specs=placed, out_specs=P(("seq", "head"), None), check_vma=False
    )
```

```python
import functools
import math

import jax
import jax.numpy as jnp
from jax import lax
from jax.experimental import pallas as pl
from jax.experimental.pallas import tpu as pltpu
from jax.sharding import PartitionSpec as P

HDIM = 128
RATIO = 4
MESH = pl.DeviceIdType.MESH
ANY = pl.BlockSpec(memory_space=pl.ANY)


def rms_scale(values_in):
    return values_in * lax.rsqrt(jnp.mean(values_in * values_in, -1, keepdims=True) + 1e-06)


def plane_width(seq_count):
    return 2 if seq_count % 2 == 0 else 1


class Plane:
    def __init__(self, seq_count, head_count):
        self.wide = plane_width(seq_count)
        self.heads = head_count
        self.size = self.wide * head_count

    def me(self):
        return lax.rem(lax.axis_index("seq"), self.wide) * self.heads + lax.axis_index("head")

    def device(self, index):
        base = lax.axis_index("seq") // self.wide * self.wide
        return (base + index // self.heads, lax.rem(index, self.heads))


class Line:
    def __init__(self, seq_count, head_count):
        self.wide = plane_width(seq_count)
        self.size = seq_count // self.wide

    def me(self):
        return lax.axis_index("seq") // self.wide

    def device(self, index):
        return (index * self.wide + lax.rem(lax.axis_index("seq"), self.wide), lax.axis_index("head"))


def greet(devices):
    barrier = pltpu.get_barrier_semaphore()
    for device in devices:
        pl.semaphore_signal(barrier, inc=1, device_id=device, device_id_type=MESH)
    pl.semaphore_wait(barrier, len(devices))


def gather_kernel(wide, length, count, *refs):
    sources, targets = [ref.at[pl.ds(1, 2)] for ref in refs[:count]], refs[count : 2 * count]
    line_send, line_recv, side_send, side_recv, own_sem = refs[2 * count :]
    seq, head = lax.axis_index("seq"), lax.axis_index("head")
    z, y = seq // wide, lax.rem(seq, wide)
    beside = [z * wide + lax.rem(y + turn, wide) for turn in range(1, wide)]
    along = [lax.rem(z + step, length) for step in range(1, length)]
    greet([(z * wide + lax.rem(y + turn, wide), head) for turn in range(1, wide)]
          + [(other * wide + y, head) for other in along])
    copies, arriving = [], []

    def begin(*ends):
        copy = remote(*ends)
        copy.start()
        return copy

    for step, other in enumerate(along):
        for item in range(count):
            arriving.append(begin(
                sources[item], targets[item].at[seq], line_send.at[item, step],
                line_recv.at[item, step], (other * wide + y, head)))
    for turn, other in enumerate(beside):
        for item in range(count):
            copies.append(begin(
                sources[item], targets[item].at[seq], side_send.at[item, turn, 0],
                side_recv.at[item, turn, 0], (other, head)))
    for item in range(count):
        own = pltpu.make_async_copy(sources[item], targets[item].at[seq], own_sem.at[item])
        own.start()
        copies.append(own)
    for step in range(length - 1):
        come = lax.rem(z + length - 1 - step, length) * wide + y
        for item in range(count):
            arriving[step * count + item].wait_recv()
            for turn, other in enumerate(beside):
                copies.append(begin(
                    targets[item].at[come], targets[item].at[come],
                    side_send.at[item, turn, step + 1], side_recv.at[item, turn, step + 1],
                    (other, head)))
    for copy in arriving:
        copy.wait_send()
    for copy in copies:
        copy.wait()


def gather_seq(number, seq_count, arrays):
    wide = plane_width(seq_count)
    length, count = seq_count // wide, len(arrays)
    return pl.pallas_call(
        functools.partial(gather_kernel, wide, length, count),
        out_shape=[jax.ShapeDtypeStruct((seq_count, 2, *a.shape[1:]), a.dtype) for a in arrays],
        in_specs=[ANY] * count,
        out_specs=[ANY] * count,
        scratch_shapes=[
            pltpu.SemaphoreType.DMA((count, length)),
            pltpu.SemaphoreType.DMA((count, length)),
            pltpu.SemaphoreType.DMA((count, wide, length)),
            pltpu.SemaphoreType.DMA((count, wide, length)),
            pltpu.SemaphoreType.DMA((count,)),
        ],
        compiler_params=pltpu.CompilerParams(collective_id=number, has_side_effects=True),
        name="gather_" + str(number),
    )(*arrays)


LANES = 128
VMEM = pl.BlockSpec(memory_space=pltpu.VMEM)


def remote(source, target, send, recv, device):
    return pltpu.make_async_remote_copy(
        src_ref=source, dst_ref=target, send_sem=send, recv_sem=recv,
        device_id=device, device_id_type=MESH,
    )


def to_row(column):
    return jnp.transpose(jnp.broadcast_to(column, (column.shape[0], LANES)))[:8]


def to_column(row):
    return jnp.transpose(jnp.broadcast_to(row, (LANES, row.shape[1])))[:, :1]


def front_kernel(
    plane, line, chunks, tokens, ids, gain, shift, normed, all_ids, seen, part, passing, sums,
    stats, parts, id_send, id_recv, seen_send, seen_recv, pass_send, pass_recv, stat_send,
    stat_recv, norm_send, norm_recv, own_sem,
):
    me, z, length = plane.me(), line.me(), line.size
    src_rows = tokens.shape[0]
    rows = part.shape[2]
    width = chunks * LANES
    feature_width = width * plane.size
    others = [lax.rem(me + step, plane.size) for step in range(1, plane.size)]
    devices = [plane.device(other) for other in others]
    above, below = lax.rem(z + 1, length), lax.rem(z + length - 1, length)
    along = [lax.rem(z + step, length) for step in range(1, length)]
    greet(devices + [line.device(other) for other in along])

    def slab(index, chunk):
        return pl.ds(pl.multiple_of(index * width + chunk * LANES, LANES), LANES)

    started = []

    def go(copy):
        copy.start()
        started.append(copy)
        return copy

    id_copies = [
        go(remote(ids, all_ids.at[me], id_send.at[step], id_recv.at[step], device))
        for step, device in enumerate(devices)
    ]
    seen_copies = [
        [
            go(remote(tokens.at[:, slab(other, chunk)], seen.at[chunk, me],
                      seen_send.at[chunk, step], seen_recv.at[chunk, step], devices[step]))
            for step, other in enumerate(others)
        ]
        for chunk in range(chunks)
    ]
    all_ids[me] = ids[...]
    for chunk in range(chunks):
        seen[chunk, me] = tokens[:, slab(me, chunk)]
    for copy in id_copies:
        copy.wait_recv()
    labels = jnp.concatenate([all_ids[index] for index in range(plane.size)], axis=1)
    places = lax.broadcasted_iota(jnp.int32, (rows, 1), 0)

    def upward(chunk, dest):
        return remote(part.at[chunk, dest], passing.at[chunk, dest + 1], pass_send.at[chunk, dest + 1],
                      pass_recv.at[chunk, dest + 1], line.device(above))

    def downward(chunk, dest):
        return remote(part.at[chunk, dest], passing.at[chunk, dest], pass_send.at[chunk, dest],
                      pass_recv.at[chunk, dest], line.device(below))

    for chunk in range(chunks):
        for copy in seen_copies[chunk]:
            copy.wait_recv()
        arrived = seen[chunk].reshape(plane.size * src_rows, LANES)
        for dest in range(length):
            chosen = (places + dest * rows == labels).astype(jnp.float32).astype(jnp.bfloat16)
            part[chunk, dest] = jnp.dot(chosen, arrived, preferred_element_type=jnp.float32)
        for turn in range(length - 1):
            high, low = length - 1 - turn, turn

            @pl.when(z < high)
            def _():
                @pl.when(z > 0)
                def _():
                    upward(chunk, high).wait_recv()
                    part[chunk, high] += passing[chunk, high + 1]
                upward(chunk, high).start()

            @pl.when(z > low)
            def _():
                @pl.when(z < length - 1)
                def _():
                    downward(chunk, low).wait_recv()
                    part[chunk, low] += passing[chunk, low]
                downward(chunk, low).start()

    for chunk in range(chunks):
        for dest in range(length):
            @pl.when(z == dest)
            def _():
                total = part[chunk, dest]
                if dest > 0:
                    upward(chunk, dest).wait_recv()
                    total = total + passing[chunk, dest + 1]
                if dest < length - 1:
                    downward(chunk, dest).wait_recv()
                    total = total + passing[chunk, dest]
                sums[:, chunk * LANES:(chunk + 1) * LANES] = total

    values = sums[...]
    part_mean = jnp.mean(values, -1, keepdims=True)
    apart = values - part_mean
    spread = jnp.sum(apart * apart, -1, keepdims=True)
    stats[me, 0:8] = to_row(part_mean)
    stats[me, 8:16] = to_row(spread)
    stat_copies = [
        go(remote(stats.at[me], stats.at[me], stat_send.at[step], stat_recv.at[step], device))
        for step, device in enumerate(devices)
    ]
    for copy in stat_copies:
        copy.wait_recv()
    means = [stats[index, 0:1] for index in range(plane.size)]
    row_mean = sum(means) * (1.0 / plane.size)
    row_var = sum([stats[index, 8:9] for index in range(plane.size)])
    for mean in means:
        row_var = row_var + width * (mean - row_mean) * (mean - row_mean)
    scale = to_column(lax.rsqrt(row_var * (1.0 / feature_width) + 1e-06))
    own = pl.ds(pl.multiple_of(me * width, LANES), width)
    parts[...] = (
        (values - to_column(row_mean)) * scale * gain[:, own] + shift[:, own]
    ).astype(jnp.bfloat16)
    merged_rows = rows // plane.wide

    def rows_of(index):
        return pl.ds(pl.multiple_of(index // plane.heads * merged_rows, merged_rows), merged_rows)

    norm_copies = [
        go(remote(parts.at[rows_of(other)], normed.at[:, own], norm_send.at[step],
                  norm_recv.at[step], devices[step]))
        for step, other in enumerate(others)
    ]
    mine = pltpu.make_async_copy(parts.at[rows_of(me)], normed.at[:, own], own_sem)
    mine.start()
    mine.wait()
    for copy in norm_copies:
        copy.wait_recv()
    for copy in started:
        copy.wait_send()
    for chunk in range(chunks):
        for dest in range(length):
            @pl.when(z < dest)
            def _():
                upward(chunk, dest).wait_send()

            @pl.when(z > dest)
            def _():
                downward(chunk, dest).wait_send()


def front(number, plane, line, tokens, ids, gain, shift):
    src_rows, feature_width = tokens.shape
    width = feature_width // plane.size
    chunks = width // LANES
    merged_rows = src_rows * plane.heads // RATIO
    rows = plane.wide * merged_rows
    dma = pltpu.SemaphoreType.DMA
    others = plane.size - 1
    return pl.pallas_call(
        functools.partial(front_kernel, plane, line, chunks),
        out_shape=[
            jax.ShapeDtypeStruct((merged_rows, feature_width), jnp.bfloat16),
            jax.ShapeDtypeStruct((plane.size, 1, src_rows), jnp.int32),
        ],
        in_specs=[VMEM] * 4,
        out_specs=[VMEM] * 2,
        scratch_shapes=[
            pltpu.VMEM((chunks, plane.size, src_rows, LANES), jnp.bfloat16),
            pltpu.VMEM((chunks, line.size, rows, LANES), jnp.float32),
            pltpu.VMEM((chunks, line.size + 1, rows, LANES), jnp.float32),
            pltpu.VMEM((rows, width), jnp.float32),
            pltpu.VMEM((plane.size, 16, rows), jnp.float32),
            pltpu.VMEM((rows, width), jnp.bfloat16),
            dma((others,)),
            dma((others,)),
            dma((chunks, others)),
            dma((chunks, others)),
            dma((chunks, line.size + 1)),
            dma((chunks, line.size + 1)),
            dma((others,)),
            dma((others,)),
            dma((others,)),
            dma((others,)),
            dma(()),
        ],
        compiler_params=pltpu.CompilerParams(
            collective_id=number, has_side_effects=True, vmem_limit_bytes=56 * 2**20
        ),
        name="front",
    )(tokens, ids, gain, shift)


def project_kernel(normed, weights, gains, out):
    made = jnp.dot(normed[...], weights[0], preferred_element_type=jnp.float32)
    plain = pl.program_id(0) == 2
    for start in range(0, made.shape[1], HDIM):
        one = made[:, start:start + HDIM]
        scaled = rms_scale(one) * gains[0]
        out[0, :, start:start + HDIM] = jnp.where(plain, one, scaled).astype(jnp.bfloat16)


def project(normed, weights, gains):
    rows, depth = normed.shape
    width = weights.shape[2]
    return pl.pallas_call(
        project_kernel,
        grid=(3,),
        out_shape=jax.ShapeDtypeStruct((3, rows, width), jnp.bfloat16),
        in_specs=[
            pl.BlockSpec((rows, depth), lambda j: (0, 0)),
            pl.BlockSpec((1, depth, width), lambda j: (j, 0, 0)),
            pl.BlockSpec((1, 1, HDIM), lambda j: (j, 0, 0)),
        ],
        out_specs=pl.BlockSpec((1, rows, width), lambda j: (j, 0, 0)),
        compiler_params=pltpu.CompilerParams(vmem_limit_bytes=56 * 2**20),
        name="project",
    )(normed, weights, gains)


def attend_kernel(mine, pairs, w_out, partial):
    rows, width = mine.shape[1], mine.shape[2]
    heads = []
    for start in range(0, width, HDIM):
        spot = slice(start, start + HDIM)
        keys = pairs[:, 0, :, spot].reshape(-1, HDIM)
        values = pairs[:, 1, :, spot].reshape(-1, HDIM)
        scores = lax.dot_general(
            mine[0, :, spot], keys, (((1,), (1,)), ((), ())), preferred_element_type=jnp.float32
        )
        expo = jnp.exp(scores - jnp.max(scores, -1, keepdims=True))
        total = jnp.sum(expo, -1, keepdims=True)
        weighted = jnp.dot(expo.astype(jnp.bfloat16), values, preferred_element_type=jnp.float32)
        heads.append((weighted / total).astype(jnp.bfloat16))
    attended = jnp.concatenate(heads, axis=1)
    partial[...] = jnp.dot(
        attended, w_out[...], preferred_element_type=jnp.float32
    ).astype(jnp.bfloat16)


def tail_kernel(
    plane, line, chunks, mine, pairs, w_out, gate, ids, out, partial, pieces, merged, chooser,
    fetched, piece_send, piece_recv, up_send, up_recv, down_send, down_recv, back_send, back_recv,
):
    me, z, length = plane.me(), line.me(), line.size
    src_rows = out.shape[0]
    rows = merged.shape[2]
    merged_rows = rows // plane.wide
    width = chunks * LANES
    others = [lax.rem(me + step, plane.size) for step in range(1, plane.size)]
    devices = [plane.device(other) for other in others]
    above, below = lax.rem(z + 1, length), lax.rem(z + length - 1, length)
    along = [lax.rem(z + step, length) for step in range(1, length)]
    greet(devices + [line.device(other) for other in along])

    def slab(index, chunk):
        return pl.ds(pl.multiple_of(index * width + chunk * LANES, LANES), LANES)

    attend_kernel(mine, pairs, w_out, partial)
    started = []

    def go(copy):
        copy.start()
        started.append(copy)
        return copy

    piece_copies = [
        [
            go(remote(partial.at[:, slab(other, chunk)], pieces.at[chunk, me],
                      piece_send.at[chunk, step], piece_recv.at[chunk, step], devices[step]))
            for step, other in enumerate(others)
        ]
        for chunk in range(chunks)
    ]
    for chunk in range(chunks):
        pieces[chunk, me] = partial[:, slab(me, chunk)]
    places = lax.broadcasted_iota(jnp.int32, (1, length * rows), 1)
    for index in range(plane.size):
        chooser[index * src_rows:(index + 1) * src_rows] = (
            (to_column(ids[index]) == places).astype(jnp.float32).astype(jnp.bfloat16)
        )

    def upward(chunk, far):
        spot = merged.at[chunk, z - far]
        return remote(spot, spot, up_send.at[chunk, far], up_recv.at[chunk, far], line.device(above))

    def downward(chunk, far):
        spot = merged.at[chunk, z + far]
        return remote(spot, spot, down_send.at[chunk, far], down_recv.at[chunk, far],
                      line.device(below))

    def came_up(chunk, far):
        spot = merged.at[chunk, z - far]
        return remote(spot, spot, up_send.at[chunk, far - 1], up_recv.at[chunk, far - 1],
                      line.device(above))

    def came_down(chunk, far):
        spot = merged.at[chunk, z + far]
        return remote(spot, spot, down_send.at[chunk, far - 1], down_recv.at[chunk, far - 1],
                      line.device(below))

    def pass_on(chunk, far):
        if far < length - 1:
            @pl.when((z >= far) & (z < length - 1))
            def _():
                upward(chunk, far).start()

            @pl.when((z + far < length) & (z > 0))
            def _():
                downward(chunk, far).start()

    for turn in range(chunks + length - 1):
        for far in range(length):
            chunk = turn - far
            if not 0 <= chunk < chunks:
                continue
            if far == 0:
                for copy in piece_copies[chunk]:
                    copy.wait_recv()
                for y in range(plane.wide):
                    total = sum(
                        [
                            pieces[chunk, y * plane.heads + head].astype(jnp.float32)
                            for head in range(plane.heads)
                        ]
                    )
                    merged[chunk, z, y * merged_rows:(y + 1) * merged_rows] = (
                        total * gate[:, slab(me, chunk)]
                    ).astype(jnp.bfloat16)
            else:
                @pl.when(z >= far)
                def _():
                    came_up(chunk, far).wait_recv()

                @pl.when(z + far < length)
                def _():
                    came_down(chunk, far).wait_recv()
            pass_on(chunk, far)
            if far == length - 1:
                fetched[chunk] = (
                    jnp.dot(
                        chooser[...],
                        merged[chunk].reshape(length * rows, LANES),
                        preferred_element_type=jnp.float32,
                    )
                    .astype(jnp.bfloat16)
                    .reshape(plane.size, src_rows, LANES)
                )
                for step, other in enumerate(others):
                    go(remote(fetched.at[chunk, other], out.at[:, slab(me, chunk)],
                              back_send.at[chunk, step], back_recv.at[chunk, step], devices[step]))
                out[:, slab(me, chunk)] = fetched[chunk, me]
    for chunk in range(chunks):
        for far in range(length - 1):
            @pl.when((z >= far) & (z < length - 1))
            def _():
                upward(chunk, far).wait_send()

            @pl.when((z + far < length) & (z > 0))
            def _():
                downward(chunk, far).wait_send()
    backs = started[len(others) * chunks:]
    for copy in backs:
        copy.wait_recv()
    for copy in started:
        copy.wait_send()


def tail(number, plane, line, made, pairs, w_out, gate, ids):
    src_rows, feature_width = ids.shape[2], w_out.shape[1]
    merged_rows = made.shape[1]
    width = feature_width // plane.size
    chunks = width // LANES
    rows = plane.wide * merged_rows
    dma = pltpu.SemaphoreType.DMA
    others = plane.size - 1
    return pl.pallas_call(
        functools.partial(tail_kernel, plane, line, chunks),
        out_shape=jax.ShapeDtypeStruct((src_rows, feature_width), jnp.bfloat16),
        in_specs=[VMEM] * 5,
        out_specs=VMEM,
        scratch_shapes=[
            pltpu.VMEM((merged_rows, feature_width), jnp.bfloat16),
            pltpu.VMEM((chunks, plane.size, merged_rows, LANES), jnp.bfloat16),
            pltpu.VMEM((chunks, line.size, rows, LANES), jnp.bfloat16),
            pltpu.VMEM((plane.size * src_rows, line.size * rows), jnp.bfloat16),
            pltpu.VMEM((chunks, plane.size, src_rows, LANES), jnp.bfloat16),
            dma((chunks, others)),
            dma((chunks, others)),
            dma((chunks, line.size)),
            dma((chunks, line.size)),
            dma((chunks, line.size)),
            dma((chunks, line.size)),
            dma((chunks, others)),
            dma((chunks, others)),
        ],
        compiler_params=pltpu.CompilerParams(
            collective_id=number, has_side_effects=True, vmem_limit_bytes=56 * 2**20
        ),
        name="tail",
    )(made, pairs, w_out, gate, ids)


def on_device(
    tokens,
    owner_shard,
    dest_slot,
    w_qkv,
    w_out,
    norm_gain,
    norm_shift,
    query_gain,
    key_gain,
    out_gate,
):
    seq_count = lax.axis_size("seq")
    head_count = lax.axis_size("head")
    src_rows, feature_width = tokens.shape
    merged_rows = src_rows * head_count // RATIO
    plane, line = Plane(seq_count, head_count), Line(seq_count, head_count)
    destination = (owner_shard[:, 0] * merged_rows + dest_slot)[None, :]
    normed, seen_ids = front(0, plane, line, tokens, destination, norm_gain[None], norm_shift[None])
    gains = jnp.stack([query_gain / math.sqrt(HDIM), key_gain, jnp.ones_like(key_gain)])
    made = project(normed, jnp.transpose(w_qkv, (1, 0, 2)), gains[:, None])
    [pairs] = gather_seq(4, seq_count, [made])
    return tail(5, plane, line, made, pairs, w_out, out_gate[None], seen_ids)


def solution(mesh):
    placed = (
        P(("seq", "head"), None),
        P(("seq", "head"), None),
        P(("seq", "head")),
        P(None, None, "head"),
        P("head", None),
        P(),
        P(),
        P(),
        P(),
        P(),
    )
    return jax.shard_map(
        on_device, mesh=mesh, in_specs=placed, out_specs=P(("seq", "head"), None), check_vma=False
    )
```
